768 devices in a mesh: region: 12 (over z), head: 64 (over x, y, core).
Axes of the slice: x: 4, y: 8, z: 12, core: 2. Of those that a mesh axis runs over, the one named last changes fastest.
Arguments:
- query: bfloat16 [98304, 2048], P(('region', 'head')), may hold values from -6 to 6
- output: bfloat16 [98304, 2048], P(('region', 'head')), may hold values from -6 to 6
- grad_out: bfloat16 [98304, 2048], P(('region', 'head')), may hold values from -6 to 6
- log_norm: float32 [32, 98304], P(None, 'region'), may hold values from 3 to 5
- global_kv: bfloat16 [1536, 4096], P('region'), may hold values from -6 to 6
- block_ids: int32 [1536, 8], P('region'), may hold values from 0 to 23, as said below
- block_counts: int32 [1536], P('region'), may hold values from 1 to 8, as said below
Outputs:
- query_grad: bfloat16 [98304, 2048], P(('region', 'head'))
- kv_grad: float32 [1536, 4096], P('region', 'head')
The draws below stay inside these ranges and needn't reach their ends.
Inputs may be any that keep to these rules, and one draw needn't show every extreme that they name: `block_ids`: each row names 8 different global blocks; entries at or beyond the row's count are ignored. `block_counts`: number of leading entries of a boundary block's intersection list that are live.
All inputs are finite; a program needn't handle non-finite values.
Results may differ from the reference program's by a relative error of at most 0.007.
Values may be sent and summed in bfloat16 or wider, within the bound.
No kernel may reach another device: no remote copies, remote signals or barrier semaphores. Data moves between devices by JAX's collectives and lax.ppermute only.
A program may use at most 64 MiB of HBM per device.

```python
import math
import jax
import jax.numpy as jnp
from jax import lax

D = 2048
HEADS = 32
HD = 64
BLOCK = 64
MAXREF = 8
RTOK = 98304
NBLK = 1536
WORLD_TILES = 24
GTOK = 1536
N_REGION = 12


def draw_block_ids(key, part):
    first_key, second_key, third_key = jax.random.split(jax.random.fold_in(key, 11), 3)
    picked_fields = jnp.arange(WORLD_TILES, dtype=jnp.int32)[None, :]
    line_position = jnp.arange(NBLK, dtype=jnp.int32)[:, None]
    sorted_standing = jax.random.randint(first_key, (NBLK, WORLD_TILES), 0, 1 << 20, dtype=jnp.int32) * WORLD_TILES + picked_fields
    topmost_line = jax.random.randint(second_key, (), 0, NBLK, dtype=jnp.int32)
    bottom_line = jax.random.randint(third_key, (), 0, NBLK, dtype=jnp.int32)
    surplus_reward = (line_position == topmost_line) & (picked_fields == WORLD_TILES - 1) | (line_position == bottom_line) & (picked_fields == 0)
    sorted_standing = sorted_standing + surplus_reward.astype(jnp.int32) * (1 << 29)
    return lax.top_k(sorted_standing, MAXREF)[1].astype(jnp.int32)


def draw_block_counts(key, part):
    first_key, second_key, third_key = jax.random.split(jax.random.fold_in(key, 23), 3)
    first_draw = jax.random.randint(first_key, (NBLK,), 0, MAXREF, dtype=jnp.int32)
    second_draw = jax.random.randint(second_key, (NBLK,), 0, MAXREF, dtype=jnp.int32)
    counts = 1 + first_draw * second_draw // (MAXREF - 1)
    full_row = jax.random.randint(third_key, (), 0, NBLK, dtype=jnp.int32)
    return jnp.where(jnp.arange(NBLK, dtype=jnp.int32) == full_row, MAXREF, counts).astype(jnp.int32)


def steps_of(own_key, extent, pieces, smallest, high):
    factor_of = 1.0
    for dim, blocks in pieces:
        draws = jax.random.uniform(jax.random.fold_in(jax.random.fold_in(own_key, 6), dim), (blocks,), jnp.float32, smallest / len(pieces), high / len(pieces))
        factor_of = factor_of * jnp.repeat(jnp.exp(draws), extent[dim] // blocks).reshape((-1,) + (1,) * (len(extent) - 1 - dim))
    return factor_of


def scatter_about(rng, shape, deviation, reach, pieces=(), kind=jnp.bfloat16):
    array = jax.random.normal(rng, shape, jnp.float32) * deviation
    if len(pieces) > 0:
        array = steps_of(rng, shape, pieces, -0.22, 0.18) * array
    return jnp.clip(array, min=-reach, max=reach).astype(kind)


def setup_inputs(seed: int = 0) -> dict:
    seeds = jax.random.split(jax.random.key(seed), 8)
    return {
        "query": scatter_about(seeds[0], (RTOK, D), 1.0, 6.0, ((0, 768),)),
        "output": scatter_about(seeds[1], (RTOK, D), 1.0, 6.0, ((0, 768),)),
        "grad_out": scatter_about(seeds[2], (RTOK, D), 1.0, 6.0, ((0, 768),)),
        "log_norm": jnp.clip(3.0 + 2.0 * jax.random.uniform(seeds[3], (HEADS, RTOK), jnp.float32) ** steps_of(seeds[3], (HEADS, RTOK), ((1, 12),), -0.2, 0.2), 3.0, 5.0),
        "global_kv": scatter_about(seeds[4], (GTOK, 2 * D), 1.0, 6.0, ((0, 12),)),
        "block_ids": draw_block_ids(jax.random.fold_in(seeds[7], 71), 0),
        "block_counts": draw_block_counts(jax.random.fold_in(seeds[7], 71), 0),
    }


def rounded(values):
    return lax.optimization_barrier(values.astype(jnp.bfloat16)).astype(jnp.float32)

def reference(query, output, grad_out, log_norm, global_kv, block_ids, block_counts):
    score_scale = 1.0 / math.sqrt(HD)
    high = lax.Precision.HIGHEST
    region_count = N_REGION
    per_region = query.shape[0] // region_count
    blocks_region = per_region // BLOCK
    global_blocks = global_kv.shape[0] // BLOCK
    kv_blocks = global_kv.astype(jnp.float32).reshape(global_blocks, BLOCK, HEADS, 2, HD)

    def shape_rows(values):
        return values.reshape(region_count, blocks_region, BLOCK, HEADS, HD)
    norm_all = log_norm.reshape(HEADS, region_count, blocks_region, BLOCK).transpose(1, 2, 0, 3)
    ids_all = block_ids.reshape(region_count, blocks_region, MAXREF)
    counts_all = block_counts.reshape(region_count, blocks_region)

    def region_step(kv_grads, inputs):
        query_rows, output_rows, grad_rows, norm_rows, ids_rows, count_rows = inputs
        query_f = query_rows.astype(jnp.float32)
        grad_f = grad_rows.astype(jnp.float32)
        row_delta = lax.optimization_barrier(jnp.sum(grad_f * output_rows.astype(jnp.float32), axis=-1)).transpose(0, 2, 1)[..., None]

        def slot_step(carry, slot_index):
            query_acc, grads_now = carry
            slot_ids = ids_rows[:, slot_index].astype(jnp.int32)
            live_rows = (slot_index < count_rows).astype(jnp.float32)
            key_block = kv_blocks[slot_ids, :, :, 0, :]
            value_block = kv_blocks[slot_ids, :, :, 1, :]
            scores = jnp.einsum('bthd,buhd->bhtu', query_f, key_block, precision=high) * score_scale
            weights = jnp.exp(scores - norm_rows[..., None]) * live_rows[:, None, None, None]
            weight_grad = jnp.einsum('bthd,buhd->bhtu', grad_f, value_block, precision=high)
            score_grad = rounded(weights * (weight_grad - row_delta))
            query_acc = query_acc + jnp.einsum('bhtu,buhd->bthd', score_grad, key_block, precision=high)
            key_grad = jnp.einsum('bhtu,bthd->buhd', score_grad, query_f, precision=high) * score_scale
            value_grad = jnp.einsum('bhtu,bthd->buhd', rounded(weights), grad_f, precision=high)
            grads_now = grads_now.at[slot_ids].add(jnp.stack([key_grad, value_grad], axis=3))
            return ((query_acc, grads_now), None)
        start = jnp.zeros((blocks_region, BLOCK, HEADS, HD), jnp.float32)
        (query_acc, kv_grads), _ = lax.scan(slot_step, (start, kv_grads), jnp.arange(MAXREF, dtype=jnp.int32))
        return (kv_grads, (query_acc * score_scale).astype(jnp.bfloat16))
    grads_start = jnp.zeros((global_blocks, BLOCK, HEADS, 2, HD), jnp.float32)
    kv_grads, query_grad = lax.scan(region_step, grads_start, (shape_rows(query), shape_rows(output), shape_rows(grad_out), norm_all, ids_all, counts_all))
    return (query_grad.reshape(query.shape[0], HEADS * HD), kv_grads.reshape(global_blocks * BLOCK, 2 * HEADS * HD))
```

```python
import jax
import jax.numpy as jnp
from jax import lax
from jax.experimental import pallas as pl
from jax.experimental.pallas import tpu as pltpu
from jax.sharding import Mesh, PartitionSpec as P

HEADS = 32
HD = 64
BLOCK = 64
SCALE = 0.125
GROUP = 4
UNROLL = 4
TAIL = 8
F32 = jnp.float32
BF16 = jnp.bfloat16


def lanes(shape):
    return lax.broadcasted_iota(jnp.int32, shape, len(shape) - 1)


def swap_halves(x):
    return pltpu.roll(x, HD, x.ndim - 1)


def pack_kernel(q_ref, g_ref, o_ref, x_ref):
    rows = q_ref.shape[0]
    width = q_ref.shape[1]
    low = lanes((rows, 128)) < HD
    row_head = lax.broadcasted_iota(jnp.int32, (HEADS, 128), 0)
    delta = jnp.zeros((HEADS, rows), F32)
    for pair in range(width // 128):
        cols = pl.ds(pair * 128, 128)
        q = q_ref[:, cols].astype(F32)
        g = g_ref[:, cols].astype(F32)
        first = jnp.where(low, q, swap_halves(g)).astype(BF16)
        second = jnp.where(low, swap_halves(q), g).astype(BF16)
        for share in range(2):
            part = slice(share * BLOCK, (share + 1) * BLOCK)
            x_ref[4 * pair + share, 0:BLOCK, :] = first[part]
            x_ref[4 * pair + 2 + share, 0:BLOCK, :] = second[part]
        product = g * o_ref[:, cols].astype(F32)
        high = product.astype(BF16)
        rest = (product - high.astype(F32)).astype(BF16)
        picks = (row_head == 2 * pair + lanes((HEADS, 128)) // HD).astype(BF16)
        dims = (((1,), (1,)), ((), ()))
        delta += lax.dot_general(picks, high, dims, preferred_element_type=F32)
        delta += lax.dot_general(picks, rest, dims, preferred_element_type=F32)
    high = delta.astype(BF16).astype(F32)
    rest = delta - high
    low = lanes((HEADS, 128)) < HD
    tails = (
        jnp.where(low, high, swap_halves(rest)),
        jnp.where(low, swap_halves(high), rest),
    )
    for head in range(HEADS):
        for share in range(2):
            row = jnp.broadcast_to(tails[share][head : head + 1], (TAIL, 128))
            x_ref[2 * head + share, BLOCK : BLOCK + TAIL, :] = row.astype(BF16)


def attention_kernel(
    ids_ref, counts_ref, share_ref, x_ref, norm_ref, kv_ref, dq_ref, dkv_ref, acc_ref, query_ref
):
    blocks = x_ref.shape[0]
    share = share_ref[0]
    low_row = lanes((1, 128)) < HD
    low = lanes((BLOCK, 128)) < HD
    half = lanes((128, 128)) < HD
    entry = lanes((1, GROUP * BLOCK)) // BLOCK

    def clear(index, carry):
        acc_ref[index] = jnp.zeros(acc_ref.shape[1:], F32)
        return carry

    lax.fori_loop(0, acc_ref.shape[0], clear, 0)

    def run_items(items, first_entry, fresh):
        staged = []
        for m in items:
            row = 2 * m + share
            count = counts_ref[row]
            ids = [ids_ref[row * 8 + first_entry + i] for i in range(GROUP)]
            x = x_ref[m, 0:BLOCK, :]
            tail = x_ref[m, BLOCK : BLOCK + TAIL, :].astype(F32)[0:1]
            delta = tail + swap_halves(tail)
            norm = norm_ref[pl.ds(m, 1), :]
            norm = jnp.where(share == 1, norm, swap_halves(norm))
            column = jnp.where(low_row, delta, norm)
            column = jnp.broadcast_to(column, (128, 128)).T
            xf = x.astype(F32)
            q_rows = jnp.where(low, xf * SCALE, 0.0)
            g_rows = jnp.where(low, 0.0, xf)
            stacked = jnp.concatenate([q_rows, g_rows], axis=0)
            left = stacked.astype(BF16)
            left_t = stacked.T.astype(BF16)
            keys = jnp.concatenate([kv_ref[i] for i in ids], axis=0)
            both = lax.dot_general(
                left, keys, (((1,), (1,)), ((), ())), preferred_element_type=F32
            )
            live = entry + first_entry < count
            staged.append((m, ids, column, left_t, keys, both, live))
        results = []
        for m, ids, column, left_t, keys, both, live in staged:
            wide = jnp.concatenate([column] * (GROUP // 2), axis=1)
            weights = jnp.where(live, jnp.exp(both[:BLOCK] - wide[BLOCK:]), 0.0)
            score_grad = (weights * (both[BLOCK:] - wide[:BLOCK])).astype(BF16)
            both_low = jnp.concatenate([score_grad, weights.astype(BF16)], axis=0)
            kv_part = jnp.dot(left_t, both_low, preferred_element_type=F32)
            query_part = jnp.dot(score_grad, keys, preferred_element_type=F32)
            results.append((m, ids, kv_part, query_part))
        for m, ids, kv_part, query_part in results:
            if fresh:
                query_ref[m] = query_part
            else:
                query_ref[m] = query_ref[m] + query_part
            for i in range(GROUP):
                tile = kv_part[:, (i // 2) * 128 : (i // 2) * 128 + 128]
                kept = jnp.where(half if i % 2 == 0 else ~half, tile, 0.0)
                acc_ref[ids[i]] = acc_ref[ids[i]] + kept

    def first_turn(step, carry):
        run_items([step * UNROLL + i for i in range(UNROLL)], 0, True)
        return carry

    lax.fori_loop(0, blocks // UNROLL, first_turn, 0)

    def second_turn(m, carry):
        @pl.when(counts_ref[2 * m + share] > GROUP)
        def _():
            run_items([m], GROUP, False)

        return carry

    lax.fori_loop(0, blocks, second_turn, 0)

    def finish_query(m, carry):
        grad = query_ref[m] * SCALE
        upper = swap_halves(grad[BLOCK // 2 :])
        dq_ref[m] = jnp.where(low[: BLOCK // 2], grad[: BLOCK // 2], upper).astype(BF16)
        return carry

    lax.fori_loop(0, blocks, finish_query, 0)

    def finish_kv(region, carry):
        first = acc_ref[2 * region]
        second = acc_ref[2 * region + 1]
        joined = jnp.where(half, first + swap_halves(first), second + swap_halves(second))
        joined = joined.astype(BF16)
        dkv_ref[2 * region] = joined[:HD]
        dkv_ref[2 * region + 1] = joined[HD:]
        return carry

    lax.fori_loop(0, acc_ref.shape[0] // 2, finish_kv, 0)


def unpack_kernel(y_ref, out_ref):
    half_rows = BLOCK // 2
    low = lanes((half_rows, 128)) < HD
    for pair in range(HEADS // 2):
        cols = pl.ds(pair * 128, 128)
        for share in range(2):
            first = y_ref[4 * pair + share].astype(F32)
            second = y_ref[4 * pair + 2 + share].astype(F32)
            base = share * BLOCK
            upper = jnp.where(low, first, swap_halves(second))
            lower = jnp.where(low, swap_halves(first), second)
            out_ref[base : base + half_rows, cols] = upper.astype(BF16)
            out_ref[base + half_rows : base + BLOCK, cols] = lower.astype(BF16)


def sum_kernel(parts_ref, out_ref):
    total = parts_ref[0].astype(F32)
    for i in range(1, parts_ref.shape[0]):
        total = total + parts_ref[i].astype(F32)
    out_ref[...] = total.T


def vmem(count):
    return [pl.BlockSpec(memory_space=pltpu.VMEM)] * count


def body(query, output, grad_out, log_norm, global_kv, block_ids, block_counts):
    members = ("chip", "core")
    chips = lax.axis_size("chip")
    cores = lax.axis_size("core")
    regions = lax.axis_size("region")
    member_count = chips * cores
    my_head = lax.axis_index("chip")
    my_share = lax.axis_index("core")
    blocks = block_ids.shape[0] // 2
    limit = pltpu.CompilerParams(vmem_limit_bytes=32 * 1024 * 1024)

    sent = pl.pallas_call(
        pack_kernel,
        out_shape=jax.ShapeDtypeStruct((member_count, BLOCK + TAIL, 128), BF16),
        in_specs=vmem(3),
        out_specs=vmem(1)[0],
        compiler_params=limit,
        name="pack",
    )(query, grad_out, output)
    received = lax.all_to_all(sent, members, split_axis=0, concat_axis=0, tiled=True)

    kv_mine = lax.dynamic_slice_in_dim(global_kv, my_head * 128, 128, 1)
    kv_whole = lax.all_gather(kv_mine, "region", axis=0, tiled=True)
    kv_blocks = kv_whole.reshape(-1, BLOCK, 2 * HD)
    norm_mine = lax.dynamic_slice_in_dim(log_norm, my_head, 1, 0).reshape(blocks, 128)
    smem = pl.BlockSpec(memory_space=pltpu.SMEM)
    global_blocks = kv_blocks.shape[0]
    dq, dkv = pl.pallas_call(
        attention_kernel,
        out_shape=(
            jax.ShapeDtypeStruct((blocks, BLOCK // 2, 128), BF16),
            jax.ShapeDtypeStruct((global_blocks, HD, 128), BF16),
        ),
        in_specs=[smem] * 3 + vmem(3),
        out_specs=tuple(vmem(2)),
        scratch_shapes=[
            pltpu.VMEM((global_blocks, 128, 128), F32),
            pltpu.VMEM((blocks, BLOCK, 128), F32),
        ],
        compiler_params=limit,
        name="attention",
    )(
        block_ids.reshape(-1),
        block_counts,
        my_share.reshape(1).astype(jnp.int32),
        received,
        norm_mine,
        kv_blocks,
    )
    returned = lax.all_to_all(dq, members, split_axis=0, concat_axis=0, tiled=True)
    parts = lax.all_to_all(dkv, ("region", "core"), split_axis=0, concat_axis=0, tiled=True)
    query_grad = pl.pallas_call(
        unpack_kernel,
        out_shape=jax.ShapeDtypeStruct(query.shape, BF16),
        in_specs=vmem(1),
        out_specs=vmem(1)[0],
        compiler_params=limit,
        name="unpack",
    )(returned)
    kv_grad = pl.pallas_call(
        sum_kernel,
        out_shape=jax.ShapeDtypeStruct((2 * BLOCK, HD), F32),
        in_specs=vmem(1),
        out_specs=vmem(1)[0],
        compiler_params=limit,
        name="sum_parts",
    )(parts)
    return (query_grad, kv_grad)


def solution(mesh):
    regions = mesh.shape["region"]
    devices = mesh.devices.reshape(regions, -1, 2)
    split = Mesh(devices, ("region", "chip", "core"))
    tokens = ("region", "chip", "core")
    in_specs = (
        P(tokens, None),
        P(tokens, None),
        P(tokens, None),
        P(None, "region"),
        P("region", None),
        P("region", None),
        P("region"),
    )
    out_specs = (P(tokens, None), P("region", ("chip", "core")))
    return jax.shard_map(body, mesh=split, in_specs=in_specs, out_specs=out_specs, check_vma=False)
```

```python
import jax
import jax.numpy as jnp
from jax import lax
from jax.experimental import pallas as pl
from jax.experimental.pallas import tpu as pltpu
from jax.sharding import Mesh, PartitionSpec as P

HEADS = 32
HD = 64
BLOCK = 64
SCALE = 0.125
GROUP = 4
UNROLL = 16
LATER_UNROLL = 8
PACK_STEPS = 4
TAIL = 8
F32 = jnp.float32
BF16 = jnp.bfloat16


def lanes(shape):
    return lax.broadcasted_iota(jnp.int32, shape, len(shape) - 1)


def swap_halves(x):
    return pltpu.roll(x, HD, x.ndim - 1)


def pack_kernel(q_ref, g_ref, o_ref, x_ref):
    rows, width = q_ref.shape
    heads = width // HD
    low = lanes((rows, 128)) < HD
    row_head = lax.broadcasted_iota(jnp.int32, (heads, 128), 0)
    delta = jnp.zeros((heads, rows), F32)
    for pair in range(heads // 2):
        cols = pl.ds(pair * 128, 128)
        q = q_ref[:, cols].astype(F32)
        g = g_ref[:, cols].astype(F32)
        first = jnp.where(low, q, swap_halves(g)).astype(BF16)
        second = jnp.where(low, swap_halves(q), g).astype(BF16)
        for share in range(2):
            part = slice(share * BLOCK, (share + 1) * BLOCK)
            x_ref[4 * pair + share, 0:BLOCK, :] = first[part]
            x_ref[4 * pair + 2 + share, 0:BLOCK, :] = second[part]
        product = g * o_ref[:, cols].astype(F32)
        high = product.astype(BF16)
        rest = (product - high.astype(F32)).astype(BF16)
        picks = (row_head == 2 * pair + lanes((heads, 128)) // HD).astype(BF16)
        dims = (((1,), (1,)), ((), ()))
        delta += lax.dot_general(picks, high, dims, preferred_element_type=F32)
        delta += lax.dot_general(picks, rest, dims, preferred_element_type=F32)
    high = delta.astype(BF16).astype(F32)
    rest = delta - high
    low = lanes((heads, 128)) < HD
    tails = (
        jnp.where(low, high, swap_halves(rest)),
        jnp.where(low, swap_halves(high), rest),
    )
    for head in range(heads):
        for share in range(2):
            row = jnp.broadcast_to(tails[share][head : head + 1], (TAIL, 128))
            x_ref[2 * head + share, BLOCK : BLOCK + TAIL, :] = row.astype(BF16)


def slot_of(region, my_region):
    ahead = lax.rem(region // 4 - my_region // 4 + 3, 3)
    low = lax.rem(region, 4) ^ lax.rem(my_region, 4)
    return lax.rem(low, 2) * 6 + low // 2 * 3 + ahead


def attention_kernel(
    ids_ref,
    counts_ref,
    place_ref,
    x_ref,
    norm_ref,
    kv_ref,
    dq_ref,
    kept_ref,
    given_ref,
    acc_ref,
    query_ref,
    later_ref,
):
    blocks = x_ref.shape[0]
    share = place_ref[0]
    my_region = place_ref[1]
    low_row = lanes((1, 128)) < HD
    low = lanes((BLOCK, 128)) < HD
    entry = lanes((1, GROUP * BLOCK)) // BLOCK

    def clear(index, carry):
        acc_ref[index] = jnp.zeros(acc_ref.shape[1:], F32)
        return carry

    lax.fori_loop(0, acc_ref.shape[0], clear, 0, unroll=4)

    def run_items(items, first_entry, fresh):
        staged = []
        for m, count in items:
            row = 2 * m + share
            ids = [ids_ref[first_entry + i, row] for i in range(GROUP)]
            tail = x_ref[m, BLOCK : BLOCK + TAIL, :].astype(F32)[0:1]
            delta = tail + swap_halves(tail)
            norm = norm_ref[pl.ds(m, 1), :]
            norm = jnp.where(share == 1, norm, swap_halves(norm))
            column = jnp.where(low_row, delta, norm)
            column = jnp.broadcast_to(column, (128, 128)).T
            x = x_ref[m, 0:BLOCK, :]
            zero = jnp.zeros_like(x)
            scaled = jnp.where(low, x * jnp.bfloat16(SCALE), zero)
            left = jnp.concatenate([scaled, jnp.where(low, zero, x)], axis=0)
            keys = jnp.concatenate([kv_ref[i] for i in ids], axis=0)
            both = lax.dot_general(
                left, keys, (((1,), (1,)), ((), ())), preferred_element_type=F32
            )
            live = entry + first_entry < count
            staged.append((m, ids, column, left, keys, both, live))
        results = []
        for m, ids, column, left, keys, both, live in staged:
            wide = jnp.concatenate([column] * (GROUP // 2), axis=1)
            weights = jnp.where(live, jnp.exp(both[:BLOCK] - wide[BLOCK:]), 0.0)
            score_grad = weights * (both[BLOCK:] - wide[:BLOCK])
            score_low = score_grad.astype(BF16)
            both_low = jnp.concatenate([score_low, weights.astype(BF16)], axis=0)
            kv_part = lax.dot_general(
                both_low, left, (((0,), (0,)), ((), ())), preferred_element_type=F32
            )
            query_part = jnp.dot(score_low, keys, preferred_element_type=F32)
            results.append((m, ids, kv_part, query_part))
        for m, ids, kv_part, query_part in results:
            if fresh:
                query_ref[m] = query_part
            else:
                query_ref[m] = query_ref[m] + query_part
            for i in range(GROUP):
                acc_ref[ids[i]] = acc_ref[ids[i]] + kv_part[i * BLOCK : (i + 1) * BLOCK]

    def first_turn(step, carry):
        base = step * UNROLL
        run_items([(base + i, counts_ref[2 * (base + i) + share]) for i in range(UNROLL)], 0, True)
        return carry

    lax.fori_loop(0, blocks // UNROLL, first_turn, 0)

    def note(m, found):
        later_ref[found] = m
        return found + (counts_ref[2 * m + share] > GROUP).astype(jnp.int32)

    later = lax.fori_loop(0, blocks, note, 0, unroll=8)

    def second_turn(step, carry):
        items = []
        for i in range(LATER_UNROLL):
            place = step * LATER_UNROLL + i
            m = later_ref[jnp.minimum(place, blocks - 1)]
            m = jnp.where(place < later, m, 0)
            items.append((m, jnp.where(place < later, counts_ref[2 * m + share], 0)))
        run_items(items, GROUP, False)
        return carry

    lax.fori_loop(0, (later + LATER_UNROLL - 1) // LATER_UNROLL, second_turn, 0)

    def finish_query(m, carry):
        grad = query_ref[m] * SCALE
        upper = swap_halves(grad[BLOCK // 2 :])
        dq_ref[m] = jnp.where(low[: BLOCK // 2], grad[: BLOCK // 2], upper).astype(BF16)
        return carry

    lax.fori_loop(0, blocks, finish_query, 0, unroll=8)

    def finish_kv(region, carry):
        first = acc_ref[2 * region]
        second = acc_ref[2 * region + 1]
        joined = jnp.concatenate([first, second], axis=0).T
        slot = slot_of(region, my_region)
        kept_ref[slot] = jnp.where(share == 0, joined[:HD], joined[HD:])
        given_ref[slot] = jnp.where(share == 0, joined[HD:], joined[:HD]).astype(BF16)
        return carry

    lax.fori_loop(0, acc_ref.shape[0] // 2, finish_kv, 0, unroll=4)


def unpack_kernel(y_ref, out_ref):
    half_rows = BLOCK // 2
    low = lanes((half_rows, 128)) < HD
    for pair in range(HEADS // 2):
        cols = pl.ds(pair * 128, 128)
        for share in range(2):
            first = y_ref[4 * pair + share].astype(F32)
            second = y_ref[4 * pair + 2 + share].astype(F32)
            base = share * BLOCK
            upper = jnp.where(low, first, swap_halves(second))
            lower = jnp.where(low, swap_halves(first), second)
            out_ref[base : base + half_rows, cols] = upper.astype(BF16)
            out_ref[base + half_rows : base + BLOCK, cols] = lower.astype(BF16)


def vmem(count):
    return [pl.BlockSpec(memory_space=pltpu.VMEM)] * count


def attention_call(ids, counts, place, received, norm, kv_blocks):
    blocks = received.shape[0]
    global_blocks = kv_blocks.shape[0]
    smem = pl.BlockSpec(memory_space=pltpu.SMEM)
    return pl.pallas_call(
        attention_kernel,
        out_shape=(
            jax.ShapeDtypeStruct((blocks, BLOCK // 2, 128), BF16),
            jax.ShapeDtypeStruct((global_blocks // 2, HD, 128), F32),
            jax.ShapeDtypeStruct((global_blocks // 2, HD, 128), BF16),
        ),
        in_specs=[smem] * 3 + vmem(3),
        out_specs=tuple(vmem(3)),
        scratch_shapes=[
            pltpu.VMEM((global_blocks, BLOCK, 128), F32),
            pltpu.VMEM((blocks, BLOCK, 128), F32),
            pltpu.SMEM((blocks + 1,), jnp.int32),
        ],
        compiler_params=pltpu.CompilerParams(vmem_limit_bytes=32 * 1024 * 1024),
        name="attention",
    )(ids, counts, place, received, norm, kv_blocks)


def body(query, output, grad_out, log_norm, global_kv, block_ids, block_counts):
    members = ("chip", "core")
    chips = lax.axis_size("chip")
    cores = lax.axis_size("core")
    regions = lax.axis_size("region")
    member_count = chips * cores
    my_head = lax.axis_index("chip")
    my_share = lax.axis_index("core")
    blocks = block_ids.shape[0] // 2
    limit = pltpu.CompilerParams(vmem_limit_bytes=32 * 1024 * 1024)

    rows, width = query.shape
    piece = pl.BlockSpec((rows, width // PACK_STEPS), lambda i: (0, i))
    sent = pl.pallas_call(
        pack_kernel,
        grid=(PACK_STEPS,),
        out_shape=jax.ShapeDtypeStruct((member_count, BLOCK + TAIL, 128), BF16),
        in_specs=[piece] * 3,
        out_specs=pl.BlockSpec(
            (member_count // PACK_STEPS, BLOCK + TAIL, 128), lambda i: (i, 0, 0)
        ),
        compiler_params=pltpu.CompilerParams(vmem_limit_bytes=60 * 1024 * 1024),
        name="pack",
    )(query, grad_out, output)
    received = lax.all_to_all(sent, members, split_axis=0, concat_axis=0, tiled=True)

    kv_mine = lax.dynamic_slice_in_dim(global_kv, my_head * 128, 128, 1)
    kv_whole = lax.all_gather(kv_mine, "region", axis=0, tiled=True)
    kv_blocks = kv_whole.reshape(-1, BLOCK, 2 * HD)
    norm_mine = lax.dynamic_slice_in_dim(log_norm, my_head, 1, 0).reshape(blocks, 128)
    dq, kept, given = attention_call(
        block_ids.T,
        block_counts,
        jnp.stack([my_share, lax.axis_index("region")]).astype(jnp.int32),
        received,
        norm_mine,
        kv_blocks,
    )
    returned = lax.all_to_all(dq, members, split_axis=0, concat_axis=0, tiled=True)
    taken = lax.ppermute(given, "core", [(0, 1), (1, 0)])
    chip_part = kept + taken.astype(F32)
    route = [(i, i ^ 1) for i in range(regions)]
    piece = lax.ppermute(chip_part[6:].astype(BF16), "region", route)
    half_part = chip_part[:6] + piece.astype(F32)
    route = [(i, i ^ 2) for i in range(regions)]
    piece = lax.ppermute(half_part[3:].astype(BF16), "region", route)
    line_part = half_part[:3] + piece.astype(F32)
    far = []
    for k in (1, 2):
        route = [(i, (i + 4 * k) % regions) for i in range(regions)]
        far.append(lax.ppermute(line_part[k].astype(BF16), "region", route))
    kv_grad = line_part[0]
    for piece in far:
        kv_grad = kv_grad + piece.astype(F32)
    query_grad = pl.pallas_call(
        unpack_kernel,
        out_shape=jax.ShapeDtypeStruct(query.shape, BF16),
        in_specs=vmem(1),
        out_specs=vmem(1)[0],
        compiler_params=limit,
        name="unpack",
    )(returned)
    return (query_grad, kv_grad.T)


def solution(mesh):
    regions = mesh.shape["region"]
    devices = mesh.devices.reshape(regions, -1, 2)
    split = Mesh(devices, ("region", "chip", "core"))
    tokens = ("region", "chip", "core")
    in_specs = (
        P(tokens, None),
        P(tokens, None),
        P(tokens, None),
        P(None, "region"),
        P("region", None),
        P("region", None),
        P("region"),
    )
    out_specs = (P(tokens, None), P("region", ("chip", "core")))
    return jax.shard_map(body, mesh=split, in_specs=in_specs, out_specs=out_specs, check_vma=False)
```

```python
import jax
import jax.numpy as jnp
from jax import lax
from jax.experimental import pallas as pl
from jax.experimental.pallas import tpu as pltpu
from jax.sharding import Mesh, PartitionSpec as P

HEADS = 32
HD = 64
BLOCK = 64
SCALE = 0.125
GROUP = 4
UNROLL = 32
LATER_UNROLL = 8
PACK_STEPS = 2
TAIL = 8
F32 = jnp.float32
BF16 = jnp.bfloat16


def lanes(shape):
    return lax.broadcasted_iota(jnp.int32, shape, len(shape) - 1)


def swap_halves(x):
    return pltpu.roll(x, HD, x.ndim - 1)


def pack_kernel(q_ref, g_ref, o_ref, x_ref):
    rows, width = q_ref.shape
    heads = width // HD
    low = lanes((rows, 128)) < HD
    row_head = lax.broadcasted_iota(jnp.int32, (heads, 128), 0)
    delta = jnp.zeros((heads, rows), F32)
    for pair in range(heads // 2):
        cols = pl.ds(pair * 128, 128)
        q = q_ref[:, cols].astype(F32)
        g = g_ref[:, cols].astype(F32)
        first = jnp.where(low, q, swap_halves(g)).astype(BF16)
        second = jnp.where(low, swap_halves(q), g).astype(BF16)
        for share in range(2):
            part = slice(share * BLOCK, (share + 1) * BLOCK)
            x_ref[4 * pair + share, 0:BLOCK, :] = first[part]
            x_ref[4 * pair + 2 + share, 0:BLOCK, :] = second[part]
        product = g * o_ref[:, cols].astype(F32)
        high = product.astype(BF16)
        rest = (product - high.astype(F32)).astype(BF16)
        picks = (row_head == 2 * pair + lanes((heads, 128)) // HD).astype(BF16)
        dims = (((1,), (1,)), ((), ()))
        delta += lax.dot_general(picks, high, dims, preferred_element_type=F32)
        delta += lax.dot_general(picks, rest, dims, preferred_element_type=F32)
    high = delta.astype(BF16).astype(F32)
    rest = delta - high
    low = lanes((heads, 128)) < HD
    tails = (
        jnp.where(low, high, swap_halves(rest)),
        jnp.where(low, swap_halves(high), rest),
    )
    for head in range(heads):
        for share in range(2):
            row = jnp.broadcast_to(tails[share][head : head + 1], (TAIL, 128))
            x_ref[2 * head + share, BLOCK : BLOCK + TAIL, :] = row.astype(BF16)


def slot_of(region, my_region):
    ahead = lax.rem(region // 4 - my_region // 4 + 3, 3)
    low = lax.rem(region, 4) ^ lax.rem(my_region, 4)
    return lax.rem(low, 2) * 6 + low // 2 * 3 + ahead


def attention_kernel(
    ids_ref,
    counts_ref,
    place_ref,
    x_ref,
    norm_ref,
    kv_ref,
    dq_ref,
    kept_ref,
    given_ref,
    acc_ref,
    query_ref,
    later_ref,
):
    blocks = x_ref.shape[0]
    share = place_ref[0]
    my_region = place_ref[1]
    low_row = lanes((1, 128)) < HD
    low = lanes((BLOCK, 128)) < HD
    entry = lanes((1, GROUP * BLOCK)) // BLOCK

    def clear(index, carry):
        acc_ref[index] = jnp.zeros(acc_ref.shape[1:], F32)
        return carry

    lax.fori_loop(0, acc_ref.shape[0], clear, 0, unroll=4)

    def run_items(items, first_entry, fresh):
        staged = []
        for m, count in items:
            row = 2 * m + share
            ids = [ids_ref[first_entry + i, row] for i in range(GROUP)]
            tail = x_ref[m, BLOCK : BLOCK + TAIL, :].astype(F32)[0:1]
            delta = tail + swap_halves(tail)
            norm = norm_ref[pl.ds(m, 1), :]
            norm = jnp.where(share == 1, norm, swap_halves(norm))
            column = jnp.where(low_row, delta, norm)
            column = jnp.broadcast_to(column, (128, 128)).T
            x = x_ref[m, 0:BLOCK, :]
            zero = jnp.zeros_like(x)
            scaled = jnp.where(low, x * jnp.bfloat16(SCALE), zero)
            left = jnp.concatenate([scaled, jnp.where(low, zero, x)], axis=0)
            keys = jnp.concatenate([kv_ref[i] for i in ids], axis=0)
            both = lax.dot_general(
                left, keys, (((1,), (1,)), ((), ())), preferred_element_type=F32
            )
            live = entry + first_entry < count
            staged.append((m, ids, column, left, keys, both, live))
        results = []
        for m, ids, column, left, keys, both, live in staged:
            wide = jnp.concatenate([column] * (GROUP // 2), axis=1)
            weights = jnp.where(live, jnp.exp(both[:BLOCK] - wide[BLOCK:]), 0.0)
            score_grad = weights * (both[BLOCK:] - wide[:BLOCK])
            score_low = score_grad.astype(BF16)
            both_low = jnp.concatenate([score_low, weights.astype(BF16)], axis=0)
            kv_part = lax.dot_general(
                both_low, left, (((0,), (0,)), ((), ())), preferred_element_type=F32
            )
            query_part = jnp.dot(score_low, keys, preferred_element_type=F32)
            results.append((m, ids, kv_part, query_part))
        for m, ids, kv_part, query_part in results:
            if not fresh:
                query_part = query_ref[m] + query_part
            query_ref[m] = query_part
            grad = query_part * SCALE
            upper = swap_halves(grad[BLOCK // 2 :])
            dq_ref[m] = jnp.where(low[: BLOCK // 2], grad[: BLOCK // 2], upper).astype(BF16)
            for i in range(GROUP):
                acc_ref[ids[i]] = acc_ref[ids[i]] + kv_part[i * BLOCK : (i + 1) * BLOCK]

    def first_turn(step, carry):
        base = step * UNROLL
        run_items([(base + i, counts_ref[2 * (base + i) + share]) for i in range(UNROLL)], 0, True)
        return carry

    lax.fori_loop(0, blocks // UNROLL, first_turn, 0)

    def note(m, found):
        later_ref[found] = m
        return found + (counts_ref[2 * m + share] > GROUP).astype(jnp.int32)

    later = lax.fori_loop(0, blocks, note, 0, unroll=8)

    def second_turn(step, carry):
        items = []
        for i in range(LATER_UNROLL):
            place = step * LATER_UNROLL + i
            m = later_ref[jnp.minimum(place, blocks - 1)]
            m = jnp.where(place < later, m, 0)
            items.append((m, jnp.where(place < later, counts_ref[2 * m + share], 0)))
        run_items(items, GROUP, False)
        return carry

    lax.fori_loop(0, (later + LATER_UNROLL - 1) // LATER_UNROLL, second_turn, 0)

    def finish_kv(region, carry):
        first = acc_ref[2 * region]
        second = acc_ref[2 * region + 1]
        joined = jnp.concatenate([first, second], axis=0).T
        slot = slot_of(region, my_region)
        kept_ref[slot] = jnp.where(share == 0, joined[:HD], joined[HD:])
        given_ref[slot] = jnp.where(share == 0, joined[HD:], joined[:HD]).astype(BF16)
        return carry

    lax.fori_loop(0, acc_ref.shape[0] // 2, finish_kv, 0, unroll=4)


def unpack_kernel(y_ref, out_ref):
    half_rows = BLOCK // 2
    low = lanes((half_rows, 128)) < HD
    for pair in range(HEADS // 2):
        cols = pl.ds(pair * 128, 128)
        for share in range(2):
            first = y_ref[4 * pair + share].astype(F32)
            second = y_ref[4 * pair + 2 + share].astype(F32)
            base = share * BLOCK
            upper = jnp.where(low, first, swap_halves(second))
            lower = jnp.where(low, swap_halves(first), second)
            out_ref[base : base + half_rows, cols] = upper.astype(BF16)
            out_ref[base + half_rows : base + BLOCK, cols] = lower.astype(BF16)


def vmem(count):
    return [pl.BlockSpec(memory_space=pltpu.VMEM)] * count


def pack_call(query, grad_out, output):
    rows, width = query.shape
    piece = pl.BlockSpec((rows, width // PACK_STEPS), lambda i: (0, i))
    return pl.pallas_call(
        pack_kernel,
        grid=(PACK_STEPS,),
        out_shape=jax.ShapeDtypeStruct((2 * HEADS, BLOCK + TAIL, 128), BF16),
        in_specs=[piece] * 3,
        out_specs=pl.BlockSpec(
            (2 * HEADS // PACK_STEPS, BLOCK + TAIL, 128), lambda i: (i, 0, 0)
        ),
        compiler_params=pltpu.CompilerParams(vmem_limit_bytes=60 * 1024 * 1024),
        name="pack",
    )(query, grad_out, output)


def attention_call(ids, counts, place, received, norm, kv_blocks):
    blocks = received.shape[0]
    global_blocks = kv_blocks.shape[0]
    smem = pl.BlockSpec(memory_space=pltpu.SMEM)
    return pl.pallas_call(
        attention_kernel,
        out_shape=(
            jax.ShapeDtypeStruct((blocks, BLOCK // 2, 128), BF16),
            jax.ShapeDtypeStruct((global_blocks // 2, HD, 128), F32),
            jax.ShapeDtypeStruct((global_blocks // 2, HD, 128), BF16),
        ),
        in_specs=[smem] * 3 + vmem(3),
        out_specs=tuple(vmem(3)),
        scratch_shapes=[
            pltpu.VMEM((global_blocks, BLOCK, 128), F32),
            pltpu.VMEM((blocks, BLOCK, 128), F32),
            pltpu.SMEM((blocks + 1,), jnp.int32),
        ],
        compiler_params=pltpu.CompilerParams(vmem_limit_bytes=32 * 1024 * 1024),
        name="attention",
    )(ids, counts, place, received, norm, kv_blocks)


def body(query, output, grad_out, log_norm, global_kv, block_ids, block_counts):
    members = ("chip", "core")
    chips = lax.axis_size("chip")
    cores = lax.axis_size("core")
    regions = lax.axis_size("region")
    member_count = chips * cores
    my_head = lax.axis_index("chip")
    my_share = lax.axis_index("core")
    blocks = block_ids.shape[0] // 2
    limit = pltpu.CompilerParams(vmem_limit_bytes=32 * 1024 * 1024)

    sent = pack_call(query, grad_out, output)
    received = lax.all_to_all(sent, members, split_axis=0, concat_axis=0, tiled=True)

    kv_mine = lax.dynamic_slice_in_dim(global_kv, my_head * 128, 128, 1)
    kv_whole = lax.all_gather(kv_mine, "region", axis=0, tiled=True)
    kv_blocks = kv_whole.reshape(-1, BLOCK, 2 * HD)
    norm_mine = lax.dynamic_slice_in_dim(log_norm, my_head, 1, 0).reshape(blocks, 128)
    dq, kept, given = attention_call(
        block_ids.T,
        block_counts,
        jnp.stack([my_share, lax.axis_index("region")]).astype(jnp.int32),
        received,
        norm_mine,
        kv_blocks,
    )
    returned = lax.all_to_all(dq, members, split_axis=0, concat_axis=0, tiled=True)
    taken = lax.ppermute(given, "core", [(0, 1), (1, 0)])
    chip_part = kept + taken.astype(F32)
    route = [(i, i ^ 1) for i in range(regions)]
    piece = lax.ppermute(chip_part[6:].astype(BF16), "region", route)
    half_part = chip_part[:6] + piece.astype(F32)
    route = [(i, i ^ 2) for i in range(regions)]
    piece = lax.ppermute(half_part[3:].astype(BF16), "region", route)
    line_part = half_part[:3] + piece.astype(F32)
    far = []
    for k in (1, 2):
        route = [(i, (i + 4 * k) % regions) for i in range(regions)]
        far.append(lax.ppermute(line_part[k].astype(BF16), "region", route))
    kv_grad = line_part[0]
    for piece in far:
        kv_grad = kv_grad + piece.astype(F32)
    query_grad = pl.pallas_call(
        unpack_kernel,
        out_shape=jax.ShapeDtypeStruct(query.shape, BF16),
        in_specs=vmem(1),
        out_specs=vmem(1)[0],
        compiler_params=limit,
        name="unpack",
    )(returned)
    return (query_grad, kv_grad.T)


def solution(mesh):
    regions = mesh.shape["region"]
    devices = mesh.devices.reshape(regions, -1, 2)
    split = Mesh(devices, ("region", "chip", "core"))
    tokens = ("region", "chip", "core")
    in_specs = (
        P(tokens, None),
        P(tokens, None),
        P(tokens, None),
        P(None, "region"),
        P("region", None),
        P("region", None),
        P("region"),
    )
    out_specs = (P(tokens, None), P("region", ("chip", "core")))
    return jax.shard_map(body, mesh=split, in_specs=in_specs, out_specs=out_specs, check_vma=False)
```

```python
import jax
import jax.numpy as jnp
from jax import lax
from jax.experimental import pallas as pl
from jax.experimental.pallas import tpu as pltpu
from jax.sharding import Mesh, PartitionSpec as P

HEADS = 32
HD = 64
BLOCK = 64
SCALE = 0.125
GROUP = 4
UNROLL = 32
LATER_UNROLL = 8
PACK_STEPS = 2
TAIL = 8
F32 = jnp.float32
BF16 = jnp.bfloat16
REGION = ("third", "hop", "step")


def lanes(shape):
    return lax.broadcasted_iota(jnp.int32, shape, len(shape) - 1)


def swap_halves(x):
    return pltpu.roll(x, HD, x.ndim - 1)


def pack_kernel(q_ref, g_ref, o_ref, x_ref):
    rows, width = q_ref.shape
    heads = width // HD
    low = lanes((rows, 128)) < HD
    row_head = lax.broadcasted_iota(jnp.int32, (heads, 128), 0)
    delta = jnp.zeros((heads, rows), F32)
    for pair in range(heads // 2):
        cols = pl.ds(pair * 128, 128)
        q = q_ref[:, cols].astype(F32)
        g = g_ref[:, cols].astype(F32)
        first = jnp.where(low, q, swap_halves(g)).astype(BF16)
        second = jnp.where(low, swap_halves(q), g).astype(BF16)
        for share in range(2):
            part = slice(share * BLOCK, (share + 1) * BLOCK)
            x_ref[4 * pair + share, 0:BLOCK, :] = first[part]
            x_ref[4 * pair + 2 + share, 0:BLOCK, :] = second[part]
        product = g * o_ref[:, cols].astype(F32)
        high = product.astype(BF16)
        rest = (product - high.astype(F32)).astype(BF16)
        picks = (row_head == 2 * pair + lanes((heads, 128)) // HD).astype(BF16)
        dims = (((1,), (1,)), ((), ()))
        delta += lax.dot_general(picks, high, dims, preferred_element_type=F32)
        delta += lax.dot_general(picks, rest, dims, preferred_element_type=F32)
    high = delta.astype(BF16).astype(F32)
    rest = delta - high
    low = lanes((heads, 128)) < HD
    tails = (
        jnp.where(low, high, swap_halves(rest)),
        jnp.where(low, swap_halves(high), rest),
    )
    for head in range(heads):
        for share in range(2):
            row = jnp.broadcast_to(tails[share][head : head + 1], (TAIL, 128))
            x_ref[2 * head + share, BLOCK : BLOCK + TAIL, :] = row.astype(BF16)


def slot_of(line, my_region):
    return (lax.rem(line, 2) ^ lax.rem(my_region // 2, 2)) * 3 + line // 2


def attention_kernel(
    ids_ref,
    counts_ref,
    place_ref,
    x_ref,
    norm_ref,
    kv_ref,
    dq_ref,
    kept_ref,
    given_ref,
    acc_ref,
    query_ref,
    later_ref,
):
    blocks = x_ref.shape[0]
    share = place_ref[0]
    my_region = place_ref[1]
    low_row = lanes((1, 128)) < HD
    low = lanes((BLOCK, 128)) < HD
    entry = lanes((1, GROUP * BLOCK)) // BLOCK

    def clear(index, carry):
        acc_ref[index] = jnp.zeros(acc_ref.shape[1:], F32)
        return carry

    lax.fori_loop(0, acc_ref.shape[0], clear, 0, unroll=4)

    def run_items(items, first_entry, fresh):
        staged = []
        for m, count in items:
            row = 2 * m + share
            ids = [ids_ref[first_entry + i, row] for i in range(GROUP)]
            tail = x_ref[m, BLOCK : BLOCK + TAIL, :].astype(F32)[0:1]
            delta = tail + swap_halves(tail)
            norm = norm_ref[pl.ds(m, 1), :]
            norm = jnp.where(share == 1, norm, swap_halves(norm))
            column = jnp.where(low_row, delta, norm)
            column = jnp.broadcast_to(column, (128, 128)).T
            x = x_ref[m, 0:BLOCK, :]
            zero = jnp.zeros_like(x)
            scaled = jnp.where(low, x * jnp.bfloat16(SCALE), zero)
            left = jnp.concatenate([scaled, jnp.where(low, zero, x)], axis=0)
            keys = jnp.concatenate([kv_ref[i] for i in ids], axis=0)
            both = lax.dot_general(
                left, keys, (((1,), (1,)), ((), ())), preferred_element_type=F32
            )
            live = entry + first_entry < count
            staged.append((m, ids, column, left, keys, both, live))
        results = []
        for m, ids, column, left, keys, both, live in staged:
            wide = jnp.concatenate([column] * (GROUP // 2), axis=1)
            weights = jnp.where(live, jnp.exp(both[:BLOCK] - wide[BLOCK:]), 0.0)
            score_grad = weights * (both[BLOCK:] - wide[:BLOCK])
            score_low = score_grad.astype(BF16)
            both_low = jnp.concatenate([score_low, weights.astype(BF16)], axis=0)
            kv_part = lax.dot_general(
                both_low, left, (((0,), (0,)), ((), ())), preferred_element_type=F32
            )
            query_part = jnp.dot(score_low, keys, preferred_element_type=F32)
            results.append((m, ids, kv_part, query_part))
        for m, ids, kv_part, query_part in results:
            if not fresh:
                query_part = query_ref[m] + query_part
            query_ref[m] = query_part
            grad = query_part * SCALE
            upper = swap_halves(grad[BLOCK // 2 :])
            dq_ref[m] = jnp.where(low[: BLOCK // 2], grad[: BLOCK // 2], upper).astype(BF16)
            for i in range(GROUP):
                acc_ref[ids[i]] = acc_ref[ids[i]] + kv_part[i * BLOCK : (i + 1) * BLOCK]

    def first_turn(step, carry):
        base = step * UNROLL
        run_items([(base + i, counts_ref[2 * (base + i) + share]) for i in range(UNROLL)], 0, True)
        return carry

    lax.fori_loop(0, blocks // UNROLL, first_turn, 0)

    def note(m, found):
        later_ref[found] = m
        return found + (counts_ref[2 * m + share] > GROUP).astype(jnp.int32)

    later = lax.fori_loop(0, blocks, note, 0, unroll=8)

    def second_turn(step, carry):
        items = []
        for i in range(LATER_UNROLL):
            place = step * LATER_UNROLL + i
            m = later_ref[jnp.minimum(place, blocks - 1)]
            m = jnp.where(place < later, m, 0)
            items.append((m, jnp.where(place < later, counts_ref[2 * m + share], 0)))
        run_items(items, GROUP, False)
        return carry

    lax.fori_loop(0, (later + LATER_UNROLL - 1) // LATER_UNROLL, second_turn, 0)

    def finish_kv(line, carry):
        slot = slot_of(line, my_region)
        lines = acc_ref.shape[0] // 4
        for other in range(2):
            region = 2 * line + (lax.rem(my_region, 2) ^ other)
            joined = jnp.concatenate([acc_ref[2 * region], acc_ref[2 * region + 1]], axis=0).T
            own_half = jnp.where(share == 0, joined[:HD], joined[HD:])
            other_half = jnp.where(share == 0, joined[HD:], joined[:HD])
            if other == 0:
                kept_ref[slot] = own_half
                kept_ref[lines + slot] = other_half
            else:
                given_ref[slot] = own_half.astype(BF16)
                given_ref[lines + slot] = other_half.astype(BF16)
        return carry

    lax.fori_loop(0, acc_ref.shape[0] // 4, finish_kv, 0, unroll=2)


def unpack_kernel(y_ref, out_ref):
    half_rows = BLOCK // 2
    low = lanes((half_rows, 128)) < HD
    for pair in range(HEADS // 2):
        cols = pl.ds(pair * 128, 128)
        for share in range(2):
            first = y_ref[4 * pair + share].astype(F32)
            second = y_ref[4 * pair + 2 + share].astype(F32)
            base = share * BLOCK
            upper = jnp.where(low, first, swap_halves(second))
            lower = jnp.where(low, swap_halves(first), second)
            out_ref[base : base + half_rows, cols] = upper.astype(BF16)
            out_ref[base + half_rows : base + BLOCK, cols] = lower.astype(BF16)


def vmem(count):
    return [pl.BlockSpec(memory_space=pltpu.VMEM)] * count


def pack_call(query, grad_out, output):
    rows, width = query.shape
    piece = pl.BlockSpec((rows, width // PACK_STEPS), lambda i: (0, i))
    return pl.pallas_call(
        pack_kernel,
        grid=(PACK_STEPS,),
        out_shape=jax.ShapeDtypeStruct((2 * HEADS, BLOCK + TAIL, 128), BF16),
        in_specs=[piece] * 3,
        out_specs=pl.BlockSpec(
            (2 * HEADS // PACK_STEPS, BLOCK + TAIL, 128), lambda i: (i, 0, 0)
        ),
        compiler_params=pltpu.CompilerParams(vmem_limit_bytes=60 * 1024 * 1024),
        name="pack",
    )(query, grad_out, output)


def attention_call(ids, counts, place, received, norm, kv_blocks):
    blocks = received.shape[0]
    global_blocks = kv_blocks.shape[0]
    smem = pl.BlockSpec(memory_space=pltpu.SMEM)
    return pl.pallas_call(
        attention_kernel,
        out_shape=(
            jax.ShapeDtypeStruct((blocks, BLOCK // 2, 128), BF16),
            jax.ShapeDtypeStruct((global_blocks // 2, HD, 128), F32),
            jax.ShapeDtypeStruct((global_blocks // 2, HD, 128), BF16),
        ),
        in_specs=[smem] * 3 + vmem(3),
        out_specs=tuple(vmem(3)),
        scratch_shapes=[
            pltpu.VMEM((global_blocks, BLOCK, 128), F32),
            pltpu.VMEM((blocks, BLOCK, 128), F32),
            pltpu.SMEM((blocks + 1,), jnp.int32),
        ],
        compiler_params=pltpu.CompilerParams(vmem_limit_bytes=32 * 1024 * 1024),
        name="attention",
    )(ids, counts, place, received, norm, kv_blocks)


def body(query, output, grad_out, log_norm, global_kv, block_ids, block_counts):
    members = ("chip", "core")
    chips = lax.axis_size("chip")
    cores = lax.axis_size("core")
    regions = lax.axis_size(REGION)
    member_count = chips * cores
    my_head = lax.axis_index("chip")
    my_share = lax.axis_index("core")
    blocks = block_ids.shape[0] // 2
    limit = pltpu.CompilerParams(vmem_limit_bytes=32 * 1024 * 1024)

    sent = pack_call(query, grad_out, output)
    received = lax.all_to_all(sent, members, split_axis=0, concat_axis=0, tiled=True)

    kv_mine = lax.dynamic_slice_in_dim(global_kv, my_head * 128, 128, 1)
    kv_whole = lax.all_gather(kv_mine, REGION, axis=0, tiled=True)
    kv_blocks = kv_whole.reshape(-1, BLOCK, 2 * HD)
    norm_mine = lax.dynamic_slice_in_dim(log_norm, my_head, 1, 0).reshape(blocks, 128)
    dq, kept, given = attention_call(
        block_ids.T,
        block_counts,
        jnp.stack([my_share, lax.axis_index(REGION)]).astype(jnp.int32),
        received,
        norm_mine,
        kv_blocks,
    )
    returned = lax.all_to_all(dq, members, split_axis=0, concat_axis=0, tiled=True)
    swap = [(0, 1), (1, 0)]
    piece = lax.ppermute(given, "step", swap)
    step_part = kept + piece.astype(F32)
    lines = regions // 2
    piece = lax.ppermute(step_part[lines:].astype(BF16), "core", swap)
    chip_part = step_part[:lines] + piece.astype(F32)
    piece = lax.ppermute(chip_part[lines // 2 :].astype(BF16), "hop", swap)
    hop_part = (chip_part[: lines // 2] + piece.astype(F32)).astype(BF16)
    parts = lax.all_gather(hop_part, "third", axis=0, tiled=False)
    mine = lax.dynamic_index_in_dim(parts, lax.axis_index("third"), axis=1, keepdims=False)
    kv_grad = jnp.sum(mine.astype(F32), axis=0)
    query_grad = pl.pallas_call(
        unpack_kernel,
        out_shape=jax.ShapeDtypeStruct(query.shape, BF16),
        in_specs=vmem(1),
        out_specs=vmem(1)[0],
        compiler_params=limit,
        name="unpack",
    )(returned)
    return (query_grad, kv_grad.T)


def solution(mesh):
    regions = mesh.shape["region"]
    devices = mesh.devices.reshape(regions // 4, 2, 2, -1, 2)
    split = Mesh(devices, (*REGION, "chip", "core"))
    tokens = (*REGION, "chip", "core")
    in_specs = (
        P(tokens, None),
        P(tokens, None),
        P(tokens, None),
        P(None, REGION),
        P(REGION, None),
        P(REGION, None),
        P(REGION),
    )
    out_specs = (P(tokens, None), P(REGION, ("chip", "core")))
    return jax.shard_map(body, mesh=split, in_specs=in_specs, out_specs=out_specs, check_vma=False)
```

```python
import jax
import jax.numpy as jnp
from jax import lax
from jax.experimental import pallas as pl
from jax.experimental.pallas import tpu as pltpu
from jax.sharding import Mesh, PartitionSpec as P

HEADS = 32
HD = 64
BLOCK = 64
SCALE = 0.125
GROUP = 4
UNROLL = 32
LATER_UNROLL = 8
PACK_STEPS = 2
TAIL = 8
F32 = jnp.float32
BF16 = jnp.bfloat16
REGION = ("third", "hop", "step")


def lanes(shape):
    return lax.broadcasted_iota(jnp.int32, shape, len(shape) - 1)


def swap_halves(x):
    return pltpu.roll(x, HD, x.ndim - 1)


def pack_kernel(q_ref, g_ref, o_ref, x_ref):
    rows, width = q_ref.shape
    heads = width // HD
    low = lanes((rows, 128)) < HD
    row_head = lax.broadcasted_iota(jnp.int32, (heads, 128), 0)
    delta = jnp.zeros((heads, rows), F32)
    for pair in range(heads // 2):
        cols = pl.ds(pair * 128, 128)
        q = q_ref[:, cols].astype(F32)
        g = g_ref[:, cols].astype(F32)
        first = jnp.where(low, q, swap_halves(g)).astype(BF16)
        second = jnp.where(low, swap_halves(q), g).astype(BF16)
        for share in range(2):
            part = slice(share * BLOCK, (share + 1) * BLOCK)
            x_ref[4 * pair + share, 0:BLOCK, :] = first[part]
            x_ref[4 * pair + 2 + share, 0:BLOCK, :] = second[part]
        product = g * o_ref[:, cols].astype(F32)
        high = product.astype(BF16)
        rest = (product - high.astype(F32)).astype(BF16)
        picks = (row_head == 2 * pair + lanes((heads, 128)) // HD).astype(BF16)
        dims = (((1,), (1,)), ((), ()))
        delta += lax.dot_general(picks, high, dims, preferred_element_type=F32)
        delta += lax.dot_general(picks, rest, dims, preferred_element_type=F32)
    high = delta.astype(BF16).astype(F32)
    rest = delta - high
    low = lanes((heads, 128)) < HD
    tails = (
        jnp.where(low, high, swap_halves(rest)),
        jnp.where(low, swap_halves(high), rest),
    )
    for head in range(heads):
        for share in range(2):
            row = jnp.broadcast_to(tails[share][head : head + 1], (TAIL, 128))
            x_ref[2 * head + share, BLOCK : BLOCK + TAIL, :] = row.astype(BF16)


def attention_kernel(
    ids_ref,
    counts_ref,
    place_ref,
    x_ref,
    norm_ref,
    kv_ref,
    dq_ref,
    kept_ref,
    one_ref,
    two_ref,
    three_ref,
    acc_ref,
    query_ref,
    later_ref,
):
    blocks = x_ref.shape[0]
    share = place_ref[0]
    my_region = place_ref[1]
    low_row = lanes((1, 128)) < HD
    low = lanes((BLOCK, 128)) < HD
    entry = lanes((1, GROUP * BLOCK)) // BLOCK

    def clear(index, carry):
        acc_ref[index] = jnp.zeros(acc_ref.shape[1:], F32)
        return carry

    lax.fori_loop(0, acc_ref.shape[0], clear, 0, unroll=4)

    def run_items(items, first_entry, fresh):
        staged = []
        for m, count in items:
            row = 2 * m + share
            ids = [ids_ref[first_entry + i, row] for i in range(GROUP)]
            tail = x_ref[m, BLOCK : BLOCK + TAIL, :].astype(F32)[0:1]
            delta = tail + swap_halves(tail)
            norm = norm_ref[pl.ds(m, 1), :]
            norm = jnp.where(share == 1, norm, swap_halves(norm))
            column = jnp.where(low_row, delta, norm)
            column = jnp.broadcast_to(column, (128, 128)).T
            x = x_ref[m, 0:BLOCK, :]
            zero = jnp.zeros_like(x)
            scaled = jnp.where(low, x * jnp.bfloat16(SCALE), zero)
            left = jnp.concatenate([scaled, jnp.where(low, zero, x)], axis=0)
            keys = jnp.concatenate([kv_ref[i] for i in ids], axis=0)
            both = lax.dot_general(
                left, keys, (((1,), (1,)), ((), ())), preferred_element_type=F32
            )
            live = entry + first_entry < count
            staged.append((m, ids, column, left, keys, both, live))
        results = []
        for m, ids, column, left, keys, both, live in staged:
            wide = jnp.concatenate([column] * (GROUP // 2), axis=1)
            weights = jnp.where(live, jnp.exp(both[:BLOCK] - wide[BLOCK:]), 0.0)
            score_grad = weights * (both[BLOCK:] - wide[:BLOCK])
            score_low = score_grad.astype(BF16)
            both_low = jnp.concatenate([score_low, weights.astype(BF16)], axis=0)
            kv_part = lax.dot_general(
                both_low, left, (((0,), (0,)), ((), ())), preferred_element_type=F32
            )
            query_part = jnp.dot(score_low, keys, preferred_element_type=F32)
            results.append((m, ids, kv_part, query_part))
        for m, ids, kv_part, query_part in results:
            if not fresh:
                query_part = query_ref[m] + query_part
            query_ref[m] = query_part
            grad = query_part * SCALE
            upper = swap_halves(grad[BLOCK // 2 :])
            dq_ref[m] = jnp.where(low[: BLOCK // 2], grad[: BLOCK // 2], upper).astype(BF16)
            for i in range(GROUP):
                acc_ref[ids[i]] = acc_ref[ids[i]] + kv_part[i * BLOCK : (i + 1) * BLOCK]

    def first_turn(step, carry):
        base = step * UNROLL
        run_items([(base + i, counts_ref[2 * (base + i) + share]) for i in range(UNROLL)], 0, True)
        return carry

    lax.fori_loop(0, blocks // UNROLL, first_turn, 0)

    def note(m, found):
        later_ref[found] = m
        return found + (counts_ref[2 * m + share] > GROUP).astype(jnp.int32)

    later = lax.fori_loop(0, blocks, note, 0, unroll=8)

    def second_turn(step, carry):
        items = []
        for i in range(LATER_UNROLL):
            place = step * LATER_UNROLL + i
            m = later_ref[jnp.minimum(place, blocks - 1)]
            m = jnp.where(place < later, m, 0)
            items.append((m, jnp.where(place < later, counts_ref[2 * m + share], 0)))
        run_items(items, GROUP, False)
        return carry

    lax.fori_loop(0, (later + LATER_UNROLL - 1) // LATER_UNROLL, second_turn, 0)

    def finish_kv(third, carry):
        thirds = acc_ref.shape[0] // 8
        for gap, part_ref in enumerate((kept_ref, one_ref, two_ref, three_ref)):
            region = 4 * third + (lax.rem(my_region, 4) ^ gap)
            joined = jnp.concatenate([acc_ref[2 * region], acc_ref[2 * region + 1]], axis=0).T
            own_half = jnp.where(share == 0, joined[:HD], joined[HD:])
            other_half = jnp.where(share == 0, joined[HD:], joined[:HD])
            part_ref[third] = own_half.astype(part_ref.dtype)
            part_ref[thirds + third] = other_half.astype(part_ref.dtype)
        return carry

    lax.fori_loop(0, acc_ref.shape[0] // 8, finish_kv, 0)


def unpack_kernel(y_ref, out_ref):
    half_rows = BLOCK // 2
    low = lanes((half_rows, 128)) < HD
    for pair in range(HEADS // 2):
        cols = pl.ds(pair * 128, 128)
        for share in range(2):
            first = y_ref[4 * pair + share].astype(F32)
            second = y_ref[4 * pair + 2 + share].astype(F32)
            base = share * BLOCK
            upper = jnp.where(low, first, swap_halves(second))
            lower = jnp.where(low, swap_halves(first), second)
            out_ref[base : base + half_rows, cols] = upper.astype(BF16)
            out_ref[base + half_rows : base + BLOCK, cols] = lower.astype(BF16)


def vmem(count):
    return [pl.BlockSpec(memory_space=pltpu.VMEM)] * count


def pack_call(query, grad_out, output):
    rows, width = query.shape
    piece = pl.BlockSpec((rows, width // PACK_STEPS), lambda i: (0, i))
    return pl.pallas_call(
        pack_kernel,
        grid=(PACK_STEPS,),
        out_shape=jax.ShapeDtypeStruct((2 * HEADS, BLOCK + TAIL, 128), BF16),
        in_specs=[piece] * 3,
        out_specs=pl.BlockSpec(
            (2 * HEADS // PACK_STEPS, BLOCK + TAIL, 128), lambda i: (i, 0, 0)
        ),
        compiler_params=pltpu.CompilerParams(vmem_limit_bytes=60 * 1024 * 1024),
        name="pack",
    )(query, grad_out, output)


def attention_call(ids, counts, place, received, norm, kv_blocks):
    blocks = received.shape[0]
    global_blocks = kv_blocks.shape[0]
    smem = pl.BlockSpec(memory_space=pltpu.SMEM)
    return pl.pallas_call(
        attention_kernel,
        out_shape=(
            jax.ShapeDtypeStruct((blocks, BLOCK // 2, 128), BF16),
            jax.ShapeDtypeStruct((global_blocks // 4, HD, 128), F32),
            *[jax.ShapeDtypeStruct((global_blocks // 4, HD, 128), BF16)] * 3,
        ),
        in_specs=[smem] * 3 + vmem(3),
        out_specs=tuple(vmem(5)),
        scratch_shapes=[
            pltpu.VMEM((global_blocks, BLOCK, 128), F32),
            pltpu.VMEM((blocks, BLOCK, 128), F32),
            pltpu.SMEM((blocks + 1,), jnp.int32),
        ],
        compiler_params=pltpu.CompilerParams(vmem_limit_bytes=32 * 1024 * 1024),
        name="attention",
    )(ids, counts, place, received, norm, kv_blocks)


def body(query, output, grad_out, log_norm, global_kv, block_ids, block_counts):
    members = ("chip", "core")
    chips = lax.axis_size("chip")
    cores = lax.axis_size("core")
    regions = lax.axis_size(REGION)
    member_count = chips * cores
    my_head = lax.axis_index("chip")
    my_share = lax.axis_index("core")
    blocks = block_ids.shape[0] // 2
    limit = pltpu.CompilerParams(vmem_limit_bytes=32 * 1024 * 1024)

    sent = pack_call(query, grad_out, output)
    received = lax.all_to_all(sent, members, split_axis=0, concat_axis=0, tiled=True)

    kv_mine = lax.dynamic_slice_in_dim(global_kv, my_head * 128, 128, 1)
    kv_whole = lax.all_gather(kv_mine, REGION, axis=0, tiled=True)
    kv_blocks = kv_whole.reshape(-1, BLOCK, 2 * HD)
    norm_mine = lax.dynamic_slice_in_dim(log_norm, my_head, 1, 0).reshape(blocks, 128)
    dq, kept, *given = attention_call(
        block_ids.T,
        block_counts,
        jnp.stack([my_share, lax.axis_index(REGION)]).astype(jnp.int32),
        received,
        norm_mine,
        kv_blocks,
    )
    returned = lax.all_to_all(dq, members, split_axis=0, concat_axis=0, tiled=True)
    near_part = kept
    for gap, piece in enumerate(given, start=1):
        route = [(i, i ^ gap) for i in range(4)]
        near_part = near_part + lax.ppermute(piece, ("hop", "step"), route).astype(F32)
    thirds = regions // 4
    piece = lax.ppermute(near_part[thirds:].astype(BF16), "core", [(0, 1), (1, 0)])
    hop_part = (near_part[:thirds] + piece.astype(F32)).astype(BF16)
    parts = lax.all_gather(hop_part, "third", axis=0, tiled=False)
    mine = lax.dynamic_index_in_dim(parts, lax.axis_index("third"), axis=1, keepdims=False)
    kv_grad = jnp.sum(mine.astype(F32), axis=0)
    query_grad = pl.pallas_call(
        unpack_kernel,
        out_shape=jax.ShapeDtypeStruct(query.shape, BF16),
        in_specs=vmem(1),
        out_specs=vmem(1)[0],
        compiler_params=limit,
        name="unpack",
    )(returned)
    return (query_grad, kv_grad.T)


def solution(mesh):
    regions = mesh.shape["region"]
    devices = mesh.devices.reshape(regions // 4, 2, 2, -1, 2)
    split = Mesh(devices, (*REGION, "chip", "core"))
    tokens = (*REGION, "chip", "core")
    in_specs = (
        P(tokens, None),
        P(tokens, None),
        P(tokens, None),
        P(None, REGION),
        P(REGION, None),
        P(REGION, None),
        P(REGION),
    )
    out_specs = (P(tokens, None), P(REGION, ("chip", "core")))
    return jax.shard_map(body, mesh=split, in_specs=in_specs, out_specs=out_specs, check_vma=False)
```

```python
import jax
import jax.numpy as jnp
from jax import lax
from jax.experimental import pallas as pl
from jax.experimental.pallas import tpu as pltpu
from jax.sharding import Mesh, PartitionSpec as P

HEADS = 32
HD = 64
BLOCK = 64
SCALE = 0.125
GROUP = 4
UNROLL = 64
LATER_UNROLL = 8
PACK_STEPS = 2
TAIL = 8
F32 = jnp.float32
BF16 = jnp.bfloat16
REGION = ("third", "hop", "step")


def lanes(shape):
    return lax.broadcasted_iota(jnp.int32, shape, len(shape) - 1)


def swap_halves(x):
    return pltpu.roll(x, HD, x.ndim - 1)


def pack_kernel(q_ref, g_ref, o_ref, x_ref):
    rows, width = q_ref.shape
    heads = width // HD
    low = lanes((rows, 128)) < HD
    row_head = lax.broadcasted_iota(jnp.int32, (heads, 128), 0)
    delta = jnp.zeros((heads, rows), F32)
    for pair in range(heads // 2):
        cols = pl.ds(pair * 128, 128)
        q = q_ref[:, cols].astype(F32)
        g = g_ref[:, cols].astype(F32)
        first = jnp.where(low, q, swap_halves(g)).astype(BF16)
        second = jnp.where(low, swap_halves(q), g).astype(BF16)
        for share in range(2):
            part = slice(share * BLOCK, (share + 1) * BLOCK)
            x_ref[4 * pair + share, 0:BLOCK, :] = first[part]
            x_ref[4 * pair + 2 + share, 0:BLOCK, :] = second[part]
        product = g * o_ref[:, cols].astype(F32)
        high = product.astype(BF16)
        rest = (product - high.astype(F32)).astype(BF16)
        picks = (row_head == 2 * pair + lanes((heads, 128)) // HD).astype(BF16)
        dims = (((1,), (1,)), ((), ()))
        delta += lax.dot_general(picks, high, dims, preferred_element_type=F32)
        delta += lax.dot_general(picks, rest, dims, preferred_element_type=F32)
    high = delta.astype(BF16).astype(F32)
    rest = delta - high
    low = lanes((heads, 128)) < HD
    tails = (
        jnp.where(low, high, swap_halves(rest)),
        jnp.where(low, swap_halves(high), rest),
    )
    for head in range(heads):
        for share in range(2):
            row = jnp.broadcast_to(tails[share][head : head + 1], (TAIL, 128))
            x_ref[2 * head + share, BLOCK : BLOCK + TAIL, :] = row.astype(BF16)


def slot_of(line, my_region):
    ahead = lax.rem(line // 2 - my_region // 4 + 3, 3)
    return (lax.rem(line, 2) ^ lax.rem(my_region // 2, 2)) * 3 + ahead


def attention_kernel(
    ids_ref,
    counts_ref,
    place_ref,
    x_ref,
    norm_ref,
    kv_ref,
    dq_ref,
    kept_ref,
    given_ref,
    acc_ref,
    query_ref,
    later_ref,
):
    blocks = x_ref.shape[0]
    share = place_ref[0]
    my_region = place_ref[1]
    low_row = lanes((1, 128)) < HD
    low = lanes((BLOCK, 128)) < HD
    entry = lanes((1, GROUP * BLOCK)) // BLOCK

    def clear(index, carry):
        acc_ref[index] = jnp.zeros(acc_ref.shape[1:], F32)
        return carry

    lax.fori_loop(0, acc_ref.shape[0], clear, 0, unroll=4)

    def run_items(items, first_entry, fresh):
        staged = []
        for m, count in items:
            row = 2 * m + share
            ids = [ids_ref[first_entry + i, row] for i in range(GROUP)]
            tail = x_ref[m, BLOCK : BLOCK + TAIL, :].astype(F32)[0:1]
            delta = tail + swap_halves(tail)
            norm = norm_ref[pl.ds(m, 1), :]
            norm = jnp.where(share == 1, norm, swap_halves(norm))
            column = jnp.where(low_row, delta, norm)
            column = jnp.broadcast_to(column, (128, 128)).T
            x = x_ref[m, 0:BLOCK, :]
            zero = jnp.zeros_like(x)
            scaled = jnp.where(low, x * jnp.bfloat16(SCALE), zero)
            left = jnp.concatenate([scaled, jnp.where(low, zero, x)], axis=0)
            keys = jnp.concatenate([kv_ref[i] for i in ids], axis=0)
            both = lax.dot_general(
                left, keys, (((1,), (1,)), ((), ())), preferred_element_type=F32
            )
            live = entry + first_entry < count
            staged.append((m, ids, column, left, keys, both, live))
        results = []
        for m, ids, column, left, keys, both, live in staged:
            wide = jnp.concatenate([column] * (GROUP // 2), axis=1)
            weights = jnp.where(live, jnp.exp(both[:BLOCK] - wide[BLOCK:]), 0.0)
            score_grad = weights * (both[BLOCK:] - wide[:BLOCK])
            score_low = score_grad.astype(BF16)
            both_low = jnp.concatenate([score_low, weights.astype(BF16)], axis=0)
            kv_part = lax.dot_general(
                both_low, left, (((0,), (0,)), ((), ())), preferred_element_type=F32
            )
            query_part = jnp.dot(score_low, keys, preferred_element_type=F32)
            results.append((m, ids, kv_part, query_part))
        for m, ids, kv_part, query_part in results:
            if not fresh:
                query_part = query_ref[m] + query_part
            query_ref[m] = query_part
            grad = query_part * SCALE
            upper = swap_halves(grad[BLOCK // 2 :])
            dq_ref[m] = jnp.where(low[: BLOCK // 2], grad[: BLOCK // 2], upper).astype(BF16)
            for i in range(GROUP):
                acc_ref[ids[i]] = acc_ref[ids[i]] + kv_part[i * BLOCK : (i + 1) * BLOCK]

    def first_turn(step, carry):
        base = step * UNROLL
        run_items([(base + i, counts_ref[2 * (base + i) + share]) for i in range(UNROLL)], 0, True)
        return carry

    lax.fori_loop(0, blocks // UNROLL, first_turn, 0)

    def note(m, found):
        later_ref[found] = m
        return found + (counts_ref[2 * m + share] > GROUP).astype(jnp.int32)

    later = lax.fori_loop(0, blocks, note, 0, unroll=8)

    def second_turn(step, carry):
        items = []
        for i in range(LATER_UNROLL):
            place = step * LATER_UNROLL + i
            m = later_ref[jnp.minimum(place, blocks - 1)]
            m = jnp.where(place < later, m, 0)
            items.append((m, jnp.where(place < later, counts_ref[2 * m + share], 0)))
        run_items(items, GROUP, False)
        return carry

    lax.fori_loop(0, (later + LATER_UNROLL - 1) // LATER_UNROLL, second_turn, 0)

    def finish_kv(line, carry):
        slot = slot_of(line, my_region)
        lines = acc_ref.shape[0] // 4
        for other in range(2):
            region = 2 * line + (lax.rem(my_region, 2) ^ other)
            joined = jnp.concatenate([acc_ref[2 * region], acc_ref[2 * region + 1]], axis=0).T
            own_half = jnp.where(share == 0, joined[:HD], joined[HD:])
            other_half = jnp.where(share == 0, joined[HD:], joined[:HD])
            if other == 0:
                kept_ref[slot] = own_half
                kept_ref[lines + slot] = other_half
            else:
                given_ref[slot] = own_half.astype(BF16)
                given_ref[lines + slot] = other_half.astype(BF16)
        return carry

    lax.fori_loop(0, acc_ref.shape[0] // 4, finish_kv, 0, unroll=2)


def unpack_kernel(y_ref, out_ref):
    half_rows = BLOCK // 2
    low = lanes((half_rows, 128)) < HD
    for pair in range(HEADS // 2):
        cols = pl.ds(pair * 128, 128)
        for share in range(2):
            first = y_ref[4 * pair + share].astype(F32)
            second = y_ref[4 * pair + 2 + share].astype(F32)
            base = share * BLOCK
            upper = jnp.where(low, first, swap_halves(second))
            lower = jnp.where(low, swap_halves(first), second)
            out_ref[base : base + half_rows, cols] = upper.astype(BF16)
            out_ref[base + half_rows : base + BLOCK, cols] = lower.astype(BF16)


def vmem(count):
    return [pl.BlockSpec(memory_space=pltpu.VMEM)] * count


def pack_call(query, grad_out, output):
    rows, width = query.shape
    piece = pl.BlockSpec((rows, width // PACK_STEPS), lambda i: (0, i))
    return pl.pallas_call(
        pack_kernel,
        grid=(PACK_STEPS,),
        out_shape=jax.ShapeDtypeStruct((2 * HEADS, BLOCK + TAIL, 128), BF16),
        in_specs=[piece] * 3,
        out_specs=pl.BlockSpec(
            (2 * HEADS // PACK_STEPS, BLOCK + TAIL, 128), lambda i: (i, 0, 0)
        ),
        compiler_params=pltpu.CompilerParams(vmem_limit_bytes=60 * 1024 * 1024),
        name="pack",
    )(query, grad_out, output)


def attention_call(ids, counts, place, received, norm, kv_blocks):
    blocks = received.shape[0]
    global_blocks = kv_blocks.shape[0]
    smem = pl.BlockSpec(memory_space=pltpu.SMEM)
    return pl.pallas_call(
        attention_kernel,
        out_shape=(
            jax.ShapeDtypeStruct((blocks, BLOCK // 2, 128), BF16),
            jax.ShapeDtypeStruct((global_blocks // 2, HD, 128), F32),
            jax.ShapeDtypeStruct((global_blocks // 2, HD, 128), BF16),
        ),
        in_specs=[smem] * 3 + vmem(3),
        out_specs=tuple(vmem(3)),
        scratch_shapes=[
            pltpu.VMEM((global_blocks, BLOCK, 128), F32),
            pltpu.VMEM((blocks, BLOCK, 128), F32),
            pltpu.SMEM((blocks + 1,), jnp.int32),
        ],
        compiler_params=pltpu.CompilerParams(vmem_limit_bytes=32 * 1024 * 1024),
        name="attention",
    )(ids, counts, place, received, norm, kv_blocks)


def body(query, output, grad_out, log_norm, global_kv, block_ids, block_counts):
    members = ("chip", "core")
    chips = lax.axis_size("chip")
    cores = lax.axis_size("core")
    regions = lax.axis_size(REGION)
    member_count = chips * cores
    my_head = lax.axis_index("chip")
    my_share = lax.axis_index("core")
    blocks = block_ids.shape[0] // 2
    limit = pltpu.CompilerParams(vmem_limit_bytes=32 * 1024 * 1024)

    sent = pack_call(query, grad_out, output)
    received = lax.all_to_all(sent, members, split_axis=0, concat_axis=0, tiled=True)

    kv_mine = lax.dynamic_slice_in_dim(global_kv, my_head * 128, 128, 1)
    kv_whole = lax.all_gather(kv_mine, REGION, axis=0, tiled=True)
    kv_blocks = kv_whole.reshape(-1, BLOCK, 2 * HD)
    norm_mine = lax.dynamic_slice_in_dim(log_norm, my_head, 1, 0).reshape(blocks, 128)
    dq, kept, given = attention_call(
        block_ids.T,
        block_counts,
        jnp.stack([my_share, lax.axis_index(REGION)]).astype(jnp.int32),
        received,
        norm_mine,
        kv_blocks,
    )
    returned = lax.all_to_all(dq, members, split_axis=0, concat_axis=0, tiled=True)
    swap = [(0, 1), (1, 0)]
    piece = lax.ppermute(given, "step", swap)
    step_part = kept + piece.astype(F32)
    lines = regions // 2
    piece = lax.ppermute(step_part[lines:].astype(BF16), "core", swap)
    chip_part = step_part[:lines] + piece.astype(F32)
    piece = lax.ppermute(chip_part[lines // 2 :].astype(BF16), "hop", swap)
    hop_part = chip_part[: lines // 2] + piece.astype(F32)
    far = []
    for k in (1, 2):
        route = [(i, (i + k) % 3) for i in range(3)]
        far.append(lax.ppermute(hop_part[k].astype(BF16), "third", route))
    query_grad = pl.pallas_call(
        unpack_kernel,
        out_shape=jax.ShapeDtypeStruct(query.shape, BF16),
        in_specs=vmem(1),
        out_specs=vmem(1)[0],
        compiler_params=limit,
        name="unpack",
    )(returned)
    query_grad, *far = lax.optimization_barrier((query_grad, *far))
    kv_grad = hop_part[0]
    for piece in far:
        kv_grad = kv_grad + piece.astype(F32)
    return (query_grad, kv_grad.T)


def solution(mesh):
    regions = mesh.shape["region"]
    devices = mesh.devices.reshape(regions // 4, 2, 2, -1, 2)
    split = Mesh(devices, (*REGION, "chip", "core"))
    tokens = (*REGION, "chip", "core")
    in_specs = (
        P(tokens, None),
        P(tokens, None),
        P(tokens, None),
        P(None, REGION),
        P(REGION, None),
        P(REGION, None),
        P(REGION),
    )
    out_specs = (P(tokens, None), P(REGION, ("chip", "core")))
    return jax.shard_map(body, mesh=split, in_specs=in_specs, out_specs=out_specs, check_vma=False)
```

```python
import jax
import jax.numpy as jnp
from jax import lax
from jax.experimental import pallas as pl
from jax.experimental.pallas import tpu as pltpu
from jax.sharding import Mesh, PartitionSpec as P

HEADS = 32
HD = 64
BLOCK = 64
SCALE = 0.125
GROUP = 4
UNROLL = 64
LATER_UNROLL = 8
PACK_STEPS = 2
TAIL = 8
F32 = jnp.float32
BF16 = jnp.bfloat16
REGION = ("third", "hop", "step")


def lanes(shape):
    return lax.broadcasted_iota(jnp.int32, shape, len(shape) - 1)


def swap_halves(x):
    return pltpu.roll(x, HD, x.ndim - 1)


def pack_kernel(q_ref, g_ref, o_ref, x_ref):
    rows, width = q_ref.shape
    heads = width // HD
    low = lanes((rows, 128)) < HD
    row_head = lax.broadcasted_iota(jnp.int32, (heads, 128), 0)
    delta = jnp.zeros((heads, rows), F32)
    for pair in range(heads // 2):
        cols = pl.ds(pair * 128, 128)
        q = q_ref[:, cols].astype(F32)
        g = g_ref[:, cols].astype(F32)
        first = jnp.where(low, q, swap_halves(g)).astype(BF16)
        second = jnp.where(low, swap_halves(q), g).astype(BF16)
        for share in range(2):
            part = slice(share * BLOCK, (share + 1) * BLOCK)
            x_ref[4 * pair + share, 0:BLOCK, :] = first[part]
            x_ref[4 * pair + 2 + share, 0:BLOCK, :] = second[part]
        product = g * o_ref[:, cols].astype(F32)
        high = product.astype(BF16)
        rest = (product - high.astype(F32)).astype(BF16)
        picks = (row_head == 2 * pair + lanes((heads, 128)) // HD).astype(BF16)
        dims = (((1,), (1,)), ((), ()))
        delta += lax.dot_general(picks, high, dims, preferred_element_type=F32)
        delta += lax.dot_general(picks, rest, dims, preferred_element_type=F32)
    high = delta.astype(BF16).astype(F32)
    rest = delta - high
    low = lanes((heads, 128)) < HD
    tails = (
        jnp.where(low, high, swap_halves(rest)),
        jnp.where(low, swap_halves(high), rest),
    )
    for head in range(heads):
        for share in range(2):
            row = jnp.broadcast_to(tails[share][head : head + 1], (TAIL, 128))
            x_ref[2 * head + share, BLOCK : BLOCK + TAIL, :] = row.astype(BF16)


def slot_of(line, my_region):
    ahead = lax.rem(line // 2 - my_region // 4 + 3, 3)
    return (lax.rem(line, 2) ^ lax.rem(my_region, 2)) * 3 + ahead


def attention_kernel(
    ids_ref,
    counts_ref,
    place_ref,
    x_ref,
    norm_ref,
    kv_ref,
    dq_ref,
    kept_ref,
    given_ref,
    acc_ref,
    query_ref,
    later_ref,
):
    blocks = x_ref.shape[0]
    share = place_ref[0]
    my_region = place_ref[1]
    low_row = lanes((1, 128)) < HD
    low = lanes((BLOCK, 128)) < HD
    entry = lanes((1, GROUP * BLOCK)) // BLOCK

    def clear(index, carry):
        acc_ref[index] = jnp.zeros(acc_ref.shape[1:], F32)
        return carry

    lax.fori_loop(0, acc_ref.shape[0], clear, 0, unroll=4)

    def run_items(items, first_entry, fresh):
        staged = []
        for m, count in items:
            row = 2 * m + share
            ids = [ids_ref[first_entry + i, row] for i in range(GROUP)]
            tail = x_ref[m, BLOCK : BLOCK + TAIL, :].astype(F32)[0:1]
            delta = tail + swap_halves(tail)
            norm = norm_ref[pl.ds(m, 1), :]
            norm = jnp.where(share == 1, norm, swap_halves(norm))
            column = jnp.where(low_row, delta, norm)
            column = jnp.broadcast_to(column, (128, 128)).T
            x = x_ref[m, 0:BLOCK, :]
            zero = jnp.zeros_like(x)
            scaled = jnp.where(low, x * jnp.bfloat16(SCALE), zero)
            left = jnp.concatenate([scaled, jnp.where(low, zero, x)], axis=0)
            keys = jnp.concatenate([kv_ref[i] for i in ids], axis=0)
            both = lax.dot_general(
                left, keys, (((1,), (1,)), ((), ())), preferred_element_type=F32
            )
            live = entry + first_entry < count
            staged.append((m, ids, column, left, keys, both, live))
        results = []
        for m, ids, column, left, keys, both, live in staged:
            wide = jnp.concatenate([column] * (GROUP // 2), axis=1)
            weights = jnp.where(live, jnp.exp(both[:BLOCK] - wide[BLOCK:]), 0.0)
            score_grad = weights * (both[BLOCK:] - wide[:BLOCK])
            score_low = score_grad.astype(BF16)
            both_low = jnp.concatenate([score_low, weights.astype(BF16)], axis=0)
            kv_part = lax.dot_general(
                both_low, left, (((0,), (0,)), ((), ())), preferred_element_type=F32
            )
            query_part = jnp.dot(score_low, keys, preferred_element_type=F32)
            results.append((m, ids, kv_part, query_part))
        for m, ids, kv_part, query_part in results:
            if not fresh:
                query_part = query_ref[m] + query_part
            query_ref[m] = query_part
            grad = query_part * SCALE
            upper = swap_halves(grad[BLOCK // 2 :])
            dq_ref[m] = jnp.where(low[: BLOCK // 2], grad[: BLOCK // 2], upper).astype(BF16)
            for i in range(GROUP):
                acc_ref[ids[i]] = acc_ref[ids[i]] + kv_part[i * BLOCK : (i + 1) * BLOCK]

    def first_turn(step, carry):
        base = step * UNROLL
        run_items([(base + i, counts_ref[2 * (base + i) + share]) for i in range(UNROLL)], 0, True)
        return carry

    lax.fori_loop(0, blocks // UNROLL, first_turn, 0)

    def note(m, found):
        later_ref[found] = m
        return found + (counts_ref[2 * m + share] > GROUP).astype(jnp.int32)

    later = lax.fori_loop(0, blocks, note, 0, unroll=8)

    def second_turn(step, carry):
        items = []
        for i in range(LATER_UNROLL):
            place = step * LATER_UNROLL + i
            m = later_ref[jnp.minimum(place, blocks - 1)]
            m = jnp.where(place < later, m, 0)
            items.append((m, jnp.where(place < later, counts_ref[2 * m + share], 0)))
        run_items(items, GROUP, False)
        return carry

    lax.fori_loop(0, (later + LATER_UNROLL - 1) // LATER_UNROLL, second_turn, 0)

    def finish_kv(line, carry):
        slot = slot_of(line, my_region)
        lines = acc_ref.shape[0] // 4
        for other in range(2):
            hop = lax.rem(my_region // 2, 2) ^ other
            region = line // 2 * 4 + hop * 2 + lax.rem(line, 2)
            joined = jnp.concatenate([acc_ref[2 * region], acc_ref[2 * region + 1]], axis=0).T
            own_half = jnp.where(share == 0, joined[:HD], joined[HD:])
            other_half = jnp.where(share == 0, joined[HD:], joined[:HD])
            if other == 0:
                kept_ref[slot] = own_half
                kept_ref[lines + slot] = other_half
            else:
                given_ref[slot] = own_half.astype(BF16)
                given_ref[lines + slot] = other_half.astype(BF16)
        return carry

    lax.fori_loop(0, acc_ref.shape[0] // 4, finish_kv, 0, unroll=2)


def unpack_kernel(y_ref, out_ref):
    half_rows = BLOCK // 2
    low = lanes((half_rows, 128)) < HD
    for pair in range(HEADS // 2):
        cols = pl.ds(pair * 128, 128)
        for share in range(2):
            first = y_ref[4 * pair + share].astype(F32)
            second = y_ref[4 * pair + 2 + share].astype(F32)
            base = share * BLOCK
            upper = jnp.where(low, first, swap_halves(second))
            lower = jnp.where(low, swap_halves(first), second)
            out_ref[base : base + half_rows, cols] = upper.astype(BF16)
            out_ref[base + half_rows : base + BLOCK, cols] = lower.astype(BF16)


def vmem(count):
    return [pl.BlockSpec(memory_space=pltpu.VMEM)] * count


def pack_call(query, grad_out, output):
    rows, width = query.shape
    piece = pl.BlockSpec((rows, width // PACK_STEPS), lambda i: (0, i))
    return pl.pallas_call(
        pack_kernel,
        grid=(PACK_STEPS,),
        out_shape=jax.ShapeDtypeStruct((2 * HEADS, BLOCK + TAIL, 128), BF16),
        in_specs=[piece] * 3,
        out_specs=pl.BlockSpec(
            (2 * HEADS // PACK_STEPS, BLOCK + TAIL, 128), lambda i: (i, 0, 0)
        ),
        compiler_params=pltpu.CompilerParams(vmem_limit_bytes=60 * 1024 * 1024),
        name="pack",
    )(query, grad_out, output)


def attention_call(ids, counts, place, received, norm, kv_blocks):
    blocks = received.shape[0]
    global_blocks = kv_blocks.shape[0]
    smem = pl.BlockSpec(memory_space=pltpu.SMEM)
    return pl.pallas_call(
        attention_kernel,
        out_shape=(
            jax.ShapeDtypeStruct((blocks, BLOCK // 2, 128), BF16),
            jax.ShapeDtypeStruct((global_blocks // 2, HD, 128), F32),
            jax.ShapeDtypeStruct((global_blocks // 2, HD, 128), BF16),
        ),
        in_specs=[smem] * 3 + vmem(3),
        out_specs=tuple(vmem(3)),
        scratch_shapes=[
            pltpu.VMEM((global_blocks, BLOCK, 128), F32),
            pltpu.VMEM((blocks, BLOCK, 128), F32),
            pltpu.SMEM((blocks + 1,), jnp.int32),
        ],
        compiler_params=pltpu.CompilerParams(vmem_limit_bytes=32 * 1024 * 1024),
        name="attention",
    )(ids, counts, place, received, norm, kv_blocks)


def body(query, output, grad_out, log_norm, global_kv, block_ids, block_counts):
    members = ("chip", "core")
    chips = lax.axis_size("chip")
    cores = lax.axis_size("core")
    regions = lax.axis_size(REGION)
    member_count = chips * cores
    my_head = lax.axis_index("chip")
    my_share = lax.axis_index("core")
    blocks = block_ids.shape[0] // 2
    limit = pltpu.CompilerParams(vmem_limit_bytes=32 * 1024 * 1024)

    sent = pack_call(query, grad_out, output)
    received = lax.all_to_all(sent, members, split_axis=0, concat_axis=0, tiled=True)

    kv_mine = lax.dynamic_slice_in_dim(global_kv, my_head * 128, 128, 1)
    kv_whole = lax.all_gather(kv_mine, REGION, axis=0, tiled=True)
    kv_blocks = kv_whole.reshape(-1, BLOCK, 2 * HD)
    norm_mine = lax.dynamic_slice_in_dim(log_norm, my_head, 1, 0).reshape(blocks, 128)
    dq, kept, given = attention_call(
        block_ids.T,
        block_counts,
        jnp.stack([my_share, lax.axis_index(REGION)]).astype(jnp.int32),
        received,
        norm_mine,
        kv_blocks,
    )
    returned = lax.all_to_all(dq, members, split_axis=0, concat_axis=0, tiled=True)
    swap = [(0, 1), (1, 0)]
    piece = lax.ppermute(given, "hop", swap)
    step_part = kept + piece.astype(F32)
    lines = regions // 2
    piece = lax.ppermute(step_part[lines:].astype(BF16), "core", swap)
    chip_part = step_part[:lines] + piece.astype(F32)
    piece = lax.ppermute(chip_part[lines // 2 :].astype(BF16), "step", swap)
    hop_part = chip_part[: lines // 2] + piece.astype(F32)
    far = []
    for k in (1, 2):
        route = [(i, (i + k) % 3) for i in range(3)]
        far.append(lax.ppermute(hop_part[k].astype(BF16), "third", route))
    query_grad = pl.pallas_call(
        unpack_kernel,
        out_shape=jax.ShapeDtypeStruct(query.shape, BF16),
        in_specs=vmem(1),
        out_specs=vmem(1)[0],
        compiler_params=limit,
        name="unpack",
    )(returned)
    query_grad, *far = lax.optimization_barrier((query_grad, *far))
    kv_grad = hop_part[0]
    for piece in far:
        kv_grad = kv_grad + piece.astype(F32)
    return (query_grad, kv_grad.T)


def solution(mesh):
    regions = mesh.shape["region"]
    devices = mesh.devices.reshape(regions // 4, 2, 2, -1, 2)
    split = Mesh(devices, (*REGION, "chip", "core"))
    tokens = (*REGION, "chip", "core")
    in_specs = (
        P(tokens, None),
        P(tokens, None),
        P(tokens, None),
        P(None, REGION),
        P(REGION, None),
        P(REGION, None),
        P(REGION),
    )
    out_specs = (P(tokens, None), P(REGION, ("chip", "core")))
    return jax.shard_map(body, mesh=split, in_specs=in_specs, out_specs=out_specs, check_vma=False)
```
